32 devices in a mesh: context: 16 (over z, x, core), tensor: 2 (over y).
Axes of the slice: x: 2, y: 2, z: 4, core: 2. Of those that a mesh axis runs over, the one named last changes fastest.
Arguments:
- query_in: bfloat16 [2, 2048, 4096], P(None, 'context', 'tensor'), may hold values from -6 to 6
- key_in: bfloat16 [2, 2048, 4096], P(None, 'context', 'tensor'), may hold values from -6 to 6
- value_in: bfloat16 [2, 2048, 4096], P(None, 'context', 'tensor'), may hold values from -6 to 6
- short_filter: float32 [3, 7, 256], P(None, None, 'tensor'), may hold values from -2.4 to 2.4
- long_filter: float32 [256, 2048], P(('tensor', 'context')), may hold values from 0 to 1
- out_weight: bfloat16 [4096, 4096], P('context', 'tensor'), may hold values from -0.09375 to 0.09375
- grad_out: bfloat16 [2, 2048, 4096], P(None, 'context', 'tensor'), may hold values from -6 to 6
Outputs:
- mixed_out: bfloat16 [2, 2048, 4096], P(None, 'context', 'tensor')
- grad_query: bfloat16 [2, 2048, 4096], P(None, 'context', 'tensor')
- grad_key: bfloat16 [2, 2048, 4096], P(None, 'context', 'tensor')
- grad_value: bfloat16 [2, 2048, 4096], P(None, 'context', 'tensor')
- grad_weight: float32 [4096, 4096], P('context', 'tensor')
- grad_long: float32 [256, 2048], P(('tensor', 'context'))
The draws below stay inside these ranges and needn't reach their ends.
All inputs are finite; a program needn't handle non-finite values.
Results may differ from the reference program's by a relative error of at most 0.015.
Values may be sent and summed in bfloat16 or wider, within the bound.
A program may use at most 128 MiB of HBM per device.

```python
import math
import jax
import jax.numpy as jnp
from jax import lax

CH = 4096
OUT = 4096
GROUP = 16
TAPS = 7
SEQS = 2
SEQUENCE_LENGTH = 2048
FILTER_GROUPS = 256


def draw_long_filter(key, part):
    random_child_keys = jax.random.split(key, 6)
    sequence_offset = jnp.arange(SEQUENCE_LENGTH, dtype=jnp.float32)[None, :]
    slow_share = 0.5
    rough_low = 0.5
    rough_high = 1.5
    is_slow = jax.random.bernoulli(random_child_keys[0], slow_share, (FILTER_GROUPS, 1))
    slow_rate = jnp.exp(jax.random.uniform(random_child_keys[1], (FILTER_GROUPS, 1), jnp.float32, math.log(0.1 / SEQUENCE_LENGTH), math.log(0.8 / SEQUENCE_LENGTH)))
    fast_rate = jnp.exp(jax.random.uniform(random_child_keys[2], (FILTER_GROUPS, 1), jnp.float32, math.log(1.0 / 50.0), math.log(1.0 / 30.0)))
    falloff_speed = jnp.where(is_slow, slow_rate, fast_rate)
    filter_jitter = jax.random.uniform(random_child_keys[3], (FILTER_GROUPS, SEQUENCE_LENGTH), jnp.float32, rough_low, rough_high)
    spike_position = jax.random.randint(random_child_keys[4], (FILTER_GROUPS, 2), 0, SEQUENCE_LENGTH)
    spike_retained = jax.random.uniform(random_child_keys[5], (FILTER_GROUPS, 2), jnp.float32, 0.5, 0.8)
    spike_values = jnp.where(sequence_offset >= spike_position[:, 0:1].astype(jnp.float32), spike_retained[:, 0:1], 1.0)
    spike_values = spike_values * jnp.where(sequence_offset >= spike_position[:, 1:2].astype(jnp.float32), spike_retained[:, 1:2], 1.0)
    signal_power = jnp.expm1(-2.0 * falloff_speed * SEQUENCE_LENGTH) / jnp.expm1(-2.0 * falloff_speed)
    filter_samples = filter_jitter * spike_values * jnp.exp(-falloff_speed * sequence_offset) / jnp.sqrt(signal_power)
    return filter_samples.astype(jnp.float32)


def raised(entries, rng, source, target, parts, factor):
    def block_of(axis_at):
        return (jnp.arange(entries.shape[axis_at]) // (entries.shape[axis_at] // parts)).reshape((-1,) + (1,) * (entries.ndim - 1 - axis_at))

    near = jax.random.permutation(rng, parts)[block_of(target)]
    second = (block_of(target) + parts // 2) % parts
    return jnp.where((block_of(source) == near) | (block_of(source) == second), factor * entries, entries)


def levels(rng, extent, cuts, least, largest):
    factor_of, own = 1.0, jax.random.fold_in(rng, 6)
    for position, blocks in cuts:
        heights = jnp.exp(jax.random.uniform(jax.random.fold_in(own, position), (blocks,), jnp.float32, least / len(cuts), largest / len(cuts)))
        factor_of = factor_of * jnp.repeat(heights, extent[position] // blocks).reshape([-1 if axis == position else 1 for axis in range(len(extent))])
    return factor_of


def normal_values(rng, shape, width, reach, shards=(), kind=jnp.bfloat16):
    array = jax.random.normal(rng, shape, jnp.float32) * width
    if len(shards) > 0:
        array = levels(rng, shape, shards, -0.22, 0.18) * array
    return jnp.clip(array, min=-reach, max=reach).astype(kind)


def noise_with(rng, dims, deviation, most, cuts, heavy, held_as=jnp.bfloat16):
    result = deviation * jax.random.normal(rng, dims, jnp.float32)
    if cuts:
        result = result * levels(rng, dims, cuts, -0.22, 0.18)
    return jnp.clip(raised(result, jax.random.fold_in(rng, 3), *heavy), -most, most).astype(held_as)


def setup_inputs(seed: int = 0) -> dict:
    keys = jax.random.split(jax.random.key(seed), 8)
    return {
        "query_in": normal_values(keys[0], (SEQS, SEQUENCE_LENGTH, CH), 1.0, 6.0, ((1, 16), (2, 2))),
        "key_in": normal_values(keys[1], (SEQS, SEQUENCE_LENGTH, CH), 1.0, 6.0, ((1, 16), (2, 2))),
        "value_in": normal_values(keys[2], (SEQS, SEQUENCE_LENGTH, CH), 1.0, 6.0, ((1, 16), (2, 2))),
        "short_filter": normal_values(keys[3], (3, TAPS, FILTER_GROUPS), 0.4, 2.4, ((2, 2),), jnp.float32),
        "long_filter": draw_long_filter(jax.random.fold_in(keys[7], 71), 0),
        "out_weight": normal_values(keys[5], (OUT, CH), CH ** -0.5, 0.09375, ((0, 16), (1, 2))),
        "grad_out": noise_with(keys[6], (SEQS, SEQUENCE_LENGTH, OUT), 1.0, 6.0, ((1, 16), (2, 2)), (1, 2, 16, 2.0)),
    }


chan_block = 256


def featurize(signal, tap_weights):
    length = signal.shape[1]
    padded = jnp.pad(signal.astype(jnp.float32), ((0, 0), (TAPS - 1, 0), (0, 0)))
    summed = jnp.zeros(signal.shape, jnp.float32)
    for offset in range(TAPS):
        lead_at = TAPS - 1 - offset
        summed = summed + tap_weights[offset] * padded[:, lead_at:lead_at + length]
    return summed


def unfeaturize(gradient, tap_weights):
    length = gradient.shape[1]
    padded = jnp.pad(gradient, ((0, 0), (0, TAPS - 1), (0, 0)))
    summed = jnp.zeros(gradient.shape, jnp.float32)
    for offset in range(TAPS):
        summed = summed + tap_weights[offset] * padded[:, offset:offset + length]
    return summed


def reference(query_in, key_in, value_in, short_filter, long_filter, out_weight, grad_out):
    transform_len = 2 * SEQUENCE_LENGTH
    grad_scale = float(SEQS * SEQUENCE_LENGTH * GROUP) ** -0.5
    grad_full = grad_out.astype(jnp.float32)
    group_block = chan_block // GROUP
    block_count = CH // chan_block

    def one_block(mixed_sum, block_index):
        chan_start = block_index * chan_block
        group_start = block_index * group_block
        query_block = lax.dynamic_slice_in_dim(query_in, chan_start, chan_block, 2)
        key_block = lax.dynamic_slice_in_dim(key_in, chan_start, chan_block, 2)
        value_block = lax.dynamic_slice_in_dim(value_in, chan_start, chan_block, 2)
        tap_weights = jnp.repeat(lax.dynamic_slice_in_dim(short_filter, group_start, group_block, 2), GROUP, axis=2).astype(jnp.float32)
        query_feat = featurize(query_block, tap_weights[0])
        key_feat = featurize(key_block, tap_weights[1])
        value_feat = featurize(value_block, tap_weights[2])
        product = (key_feat * value_feat).astype(jnp.bfloat16)
        kernel = lax.dynamic_slice_in_dim(long_filter, group_start, group_block, 0).astype(jnp.float32)
        kernel_spec = jnp.repeat(jnp.fft.rfft(kernel, n=transform_len, axis=1), GROUP, axis=0).T
        product_spec = jnp.fft.rfft(product.astype(jnp.float32), n=transform_len, axis=1)
        conv_out = jnp.fft.irfft(product_spec * kernel_spec, n=transform_len, axis=1)[:, :SEQUENCE_LENGTH].astype(jnp.bfloat16)
        gated = (query_feat * conv_out.astype(jnp.float32)).astype(jnp.bfloat16)
        weight_block = lax.dynamic_slice_in_dim(out_weight, chan_start, chan_block, 1).astype(jnp.float32)
        mixed_sum = mixed_sum + jnp.einsum('blc,oc->blo', gated.astype(jnp.float32), weight_block)
        grad_gated = jnp.einsum('blo,oc->blc', grad_full, weight_block)
        grad_conv = (grad_gated * query_feat).astype(jnp.bfloat16)
        grad_weight = jnp.einsum('blo,blc->oc', grad_full, gated.astype(jnp.float32))
        conv_spec = jnp.fft.rfft(grad_conv.astype(jnp.float32), n=transform_len, axis=1)
        grad_product = jnp.fft.irfft(conv_spec * jnp.conj(kernel_spec), n=transform_len, axis=1)[:, :SEQUENCE_LENGTH].astype(jnp.bfloat16)
        crossed = jnp.sum(conv_spec * jnp.conj(product_spec), axis=0)
        crossed = jnp.sum(crossed.reshape(SEQUENCE_LENGTH + 1, group_block, GROUP), axis=2)
        grad_long = jnp.fft.irfft(crossed, n=transform_len, axis=0)[:SEQUENCE_LENGTH].T * grad_scale
        grad_qfeat = grad_gated * conv_out.astype(jnp.float32)
        grad_kfeat = grad_product.astype(jnp.float32) * value_feat
        grad_vfeat = grad_product.astype(jnp.float32) * key_feat
        grad_query = unfeaturize(grad_qfeat, tap_weights[0]).astype(jnp.bfloat16)
        grad_key = unfeaturize(grad_kfeat, tap_weights[1]).astype(jnp.bfloat16)
        grad_value = unfeaturize(grad_vfeat, tap_weights[2]).astype(jnp.bfloat16)
        return mixed_sum, (grad_query, grad_key, grad_value, grad_weight, grad_long)

    mixed_sum, stacked = lax.scan(one_block, jnp.zeros((SEQS, SEQUENCE_LENGTH, OUT), jnp.float32), jnp.arange(block_count, dtype=jnp.int32))
    grad_query = jnp.moveaxis(stacked[0], 0, 2).reshape(SEQS, SEQUENCE_LENGTH, CH)
    grad_key = jnp.moveaxis(stacked[1], 0, 2).reshape(SEQS, SEQUENCE_LENGTH, CH)
    grad_value = jnp.moveaxis(stacked[2], 0, 2).reshape(SEQS, SEQUENCE_LENGTH, CH)
    grad_weight = jnp.moveaxis(stacked[3], 0, 1).reshape(OUT, CH)
    grad_long = stacked[4].reshape(FILTER_GROUPS, SEQUENCE_LENGTH)
    return (mixed_sum.astype(jnp.bfloat16), grad_query, grad_key, grad_value, grad_weight, grad_long)
```

```python
import functools

import jax
import jax.numpy as jnp
from jax import lax
from jax.experimental import pallas as pl
from jax.experimental.pallas import tpu as pltpu
from jax.sharding import PartitionSpec as P

GROUP = 16
TAPS = 7
BLOCK = 256
HALF = 128
VMEM_LIMIT = 60 * 1024 * 1024


def shifted(value, axis, steps):
    count = lax.axis_size(axis)
    first, last = (max(0, -steps), min(count, count - steps))
    return lax.ppermute(value, axis, [(source, source + steps) for source in range(first, last)])


def whole_vmem(count):
    return [pl.BlockSpec(memory_space=pltpu.VMEM)] * count


def band_kernel(filter_ref, band_ref):
    groups, length = filter_ref.shape
    zeros = jnp.zeros((HALF, HALF), jnp.float32)

    def one_group(g, carry):
        row = jnp.broadcast_to(filter_ref[pl.ds(g, 1), :], (HALF, length))
        padded = jnp.concatenate([row, zeros], axis=1)
        rolled = pltpu.roll(padded, 0, 1, stride=1, stride_axis=0).astype(jnp.bfloat16)
        band_ref[g, 0:HALF, :] = rolled[:, :length]
        band_ref[g, HALF:BLOCK, :] = jnp.concatenate(
            [jnp.zeros((HALF, HALF), jnp.bfloat16), rolled[:, : length - HALF]], axis=1
        )
        return carry

    lax.fori_loop(0, groups, one_group, 0)


def make_band(long_filter):
    groups, length = long_filter.shape
    return pl.pallas_call(
        band_kernel,
        out_shape=jax.ShapeDtypeStruct((groups, BLOCK, length), jnp.bfloat16),
        in_specs=whole_vmem(1),
        out_specs=pl.BlockSpec(memory_space=pltpu.VMEM),
        compiler_params=pltpu.CompilerParams(vmem_limit_bytes=VMEM_LIMIT),
        cost_estimate=pl.CostEstimate(
            flops=0, bytes_accessed=groups * BLOCK * length * 2, transcendentals=0
        ),
        name="band",
    )(long_filter)


def exchange_matrix():
    row = lax.broadcasted_iota(jnp.int32, (BLOCK, BLOCK), 0)
    column = lax.broadcasted_iota(jnp.int32, (BLOCK, BLOCK), 1)
    return jnp.where(row + column == BLOCK - 1, 1.0, 0.0).astype(jnp.bfloat16)


def group_mask(g, rows, columns, channels):
    lane = lax.broadcasted_iota(jnp.int32, (rows, columns), 1)
    return (lane % channels) // GROUP == g


def correlate(band_ref, work_ref, total_ref, groups, channels):
    length, columns = work_ref.shape
    blocks = length // BLOCK
    total_ref[...] = jnp.zeros_like(total_ref)

    def one_group(g, carry):
        mask = group_mask(g, 1, columns, channels).astype(jnp.bfloat16)
        masked = work_ref[...] * mask
        for j in range(blocks):
            rows = slice(j * BLOCK, (j + 1) * BLOCK)
            total_ref[rows, :] += jnp.dot(
                band_ref[g, :, : (blocks - j) * BLOCK],
                masked[j * BLOCK :, :],
                preferred_element_type=jnp.float32,
            )
        return carry

    lax.fori_loop(0, groups, one_group, 0)


def load_block(source_ref, j):
    batches, local_rows, channels = source_ref.shape[1:]
    first, count = j * BLOCK // local_rows, BLOCK // local_rows
    return jnp.concatenate(
        [
            source_ref[first : first + count, b].reshape(BLOCK, channels)
            for b in range(batches)
        ],
        axis=1,
    )


def store_block(target_ref, j, value):
    batches, local_rows, channels = target_ref.shape[1:]
    first, count = j * BLOCK // local_rows, BLOCK // local_rows
    for b in range(batches):
        target_ref[first : first + count, b] = value[
            :, b * channels : (b + 1) * channels
        ].reshape(count, local_rows, channels)


def forward_kernel(band_ref, product_ref, out_ref, work_ref, total_ref):
    groups = band_ref.shape[0]
    length, channels = work_ref.shape[0], product_ref.shape[3]
    blocks = length // BLOCK
    exchange = exchange_matrix()
    for j in range(blocks):
        block = load_block(product_ref, j)
        mirror = slice((blocks - 1 - j) * BLOCK, (blocks - j) * BLOCK)
        work_ref[mirror, :] = jnp.dot(
            exchange, block, preferred_element_type=jnp.float32
        ).astype(jnp.bfloat16)
    correlate(band_ref, work_ref, total_ref, groups, channels)
    for j in range(blocks):
        mirror = slice((blocks - 1 - j) * BLOCK, (blocks - j) * BLOCK)
        rounded = total_ref[mirror, :].astype(jnp.bfloat16)
        value = jnp.dot(exchange, rounded, preferred_element_type=jnp.float32)
        store_block(out_ref, j, value.astype(jnp.bfloat16))


def backward_kernel(band_ref, grad_ref, out_ref, work_ref, total_ref):
    groups = band_ref.shape[0]
    length, channels = work_ref.shape[0], grad_ref.shape[3]
    blocks = length // BLOCK
    for j in range(blocks):
        rows = slice(j * BLOCK, (j + 1) * BLOCK)
        work_ref[rows, :] = load_block(grad_ref, j)
    correlate(band_ref, work_ref, total_ref, groups, channels)
    for j in range(blocks):
        rows = slice(j * BLOCK, (j + 1) * BLOCK)
        store_block(out_ref, j, total_ref[rows, :].astype(jnp.bfloat16))


def long_grad_kernel(scale, grad_ref, product_ref, out_ref, grad_work, product_work, sums):
    groups, length = out_ref.shape
    channels = grad_ref.shape[3]
    blocks = length // BLOCK
    wide = grad_work.shape[1] // blocks
    exchange = exchange_matrix()
    for j in range(blocks):
        columns = slice(j * wide, (j + 1) * wide)
        grad_work[:, columns] = load_block(grad_ref, j)
        product_work[:, columns] = jnp.dot(
            exchange, load_block(product_ref, j), preferred_element_type=jnp.float32
        ).astype(jnp.bfloat16)
    sums[:, length:] = jnp.zeros_like(sums[:, length:])

    def one_group(g, carry):
        mask = group_mask(g, 1, blocks * wide, channels).astype(jnp.bfloat16)
        masked = product_work[...] * mask
        for d in range(blocks):
            sums[:, d * BLOCK : (d + 1) * BLOCK] = lax.dot_general(
                grad_work[:, d * wide :],
                masked[:, : (blocks - d) * wide],
                (((1,), (1,)), ((), ())),
                preferred_element_type=jnp.float32,
            )
        low = sums[0:HALF, :]
        high = sums[HALF:BLOCK, :]
        folded = low + jnp.concatenate(
            [jnp.zeros((HALF, HALF), jnp.float32), high[:, : length + BLOCK - HALF]], axis=1
        )
        rolled = pltpu.roll(folded, 0, 1, stride=1, stride_axis=0)
        summed = jnp.sum(rolled, axis=0, keepdims=True)
        placed = pltpu.roll(
            jnp.broadcast_to(summed, (8, length + BLOCK)), length + 1, 1
        )
        out_ref[pl.ds(g, 1), :] = placed[0:1, :length] * scale
        return carry

    lax.fori_loop(0, groups, one_group, 0)


def correlation_call(kernel, name, band, signal):
    owners, batches, local_rows, channels = signal.shape
    length = owners * local_rows
    groups = band.shape[0]
    columns = batches * channels
    return pl.pallas_call(
        kernel,
        out_shape=jax.ShapeDtypeStruct(signal.shape, jnp.bfloat16),
        in_specs=whole_vmem(2),
        out_specs=pl.BlockSpec(memory_space=pltpu.VMEM),
        scratch_shapes=[
            pltpu.VMEM((length, columns), jnp.bfloat16),
            pltpu.VMEM((length, columns), jnp.float32),
        ],
        compiler_params=pltpu.CompilerParams(vmem_limit_bytes=VMEM_LIMIT),
        cost_estimate=pl.CostEstimate(
            flops=groups * length * length * columns,
            bytes_accessed=band.size * 2 + signal.size * 4,
            transcendentals=0,
        ),
        name=name,
    )(band, signal)


def long_grad_call(grad, product, groups, scale):
    owners, batches, local_rows, channels = grad.shape
    length = owners * local_rows
    blocks = length // BLOCK
    columns = batches * channels
    return pl.pallas_call(
        functools.partial(long_grad_kernel, scale),
        out_shape=jax.ShapeDtypeStruct((groups, length), jnp.float32),
        in_specs=whole_vmem(2),
        out_specs=pl.BlockSpec(memory_space=pltpu.VMEM),
        scratch_shapes=[
            pltpu.VMEM((BLOCK, blocks * columns), jnp.bfloat16),
            pltpu.VMEM((BLOCK, blocks * columns), jnp.bfloat16),
            pltpu.VMEM((BLOCK, length + BLOCK), jnp.float32),
        ],
        compiler_params=pltpu.CompilerParams(vmem_limit_bytes=VMEM_LIMIT),
        cost_estimate=pl.CostEstimate(
            flops=groups * length * length * columns,
            bytes_accessed=grad.size * 4 + groups * length * 4,
            transcendentals=0,
        ),
        name="long_grad",
    )(grad, product)


def featurize(signal, leading, tap_weights):
    local_rows = signal.shape[1]
    padded = jnp.concatenate([leading, signal], axis=1)
    summed = jnp.zeros(signal.shape, jnp.float32)
    for offset in range(TAPS):
        lead_at = TAPS - 1 - offset
        summed = summed + tap_weights[offset] * padded[:, lead_at : lead_at + local_rows].astype(
            jnp.float32
        )
    return summed


def unfeaturize(gradient, trailing, tap_weights):
    local_rows = gradient.shape[1]
    padded = jnp.concatenate([gradient, trailing], axis=1)
    summed = jnp.zeros(gradient.shape, jnp.float32)
    for offset in range(TAPS):
        summed = summed + tap_weights[offset] * padded[:, offset : offset + local_rows]
    return summed


def to_owners(value, axis):
    count = lax.axis_size(axis)
    batches, rows, channels = value.shape
    split = value.reshape(batches, rows, count, channels // count).transpose(2, 0, 1, 3)
    return lax.all_to_all(split, axis, split_axis=0, concat_axis=0, tiled=True)


def from_owners(value, axis):
    owners, batches, rows, channels = value.shape
    back = lax.all_to_all(value, axis, split_axis=0, concat_axis=0, tiled=True)
    return back.transpose(1, 2, 0, 3).reshape(batches, rows, owners * channels)


def gather_features(value, axis):
    count = lax.axis_size(axis)
    me = lax.axis_index(axis)
    width = value.shape[2]
    gathered = jnp.zeros(value.shape[:2] + (count * width,), value.dtype)
    for step in range(count):
        part = value
        if step:
            pairs = [(source, (source - step) % count) for source in range(count)]
            part = lax.ppermute(value, axis, pairs)
        gathered = lax.dynamic_update_slice_in_dim(
            gathered, part, (me + step) % count * width, 2
        )
    return gathered


def scatter_features(value, axis):
    count = lax.axis_size(axis)
    me = lax.axis_index(axis)
    width = value.shape[2] // count
    total = lax.dynamic_slice_in_dim(value, me * width, width, 2).astype(jnp.float32)
    for step in range(1, count):
        part = lax.dynamic_slice_in_dim(value, (me + step) % count * width, width, 2)
        pairs = [(source, (source + step) % count) for source in range(count)]
        total = total + lax.ppermute(part.astype(jnp.bfloat16), axis, pairs).astype(jnp.float32)
    return total.astype(jnp.bfloat16)


def body(query_in, key_in, value_in, short_filter, long_filter, out_weight, grad_out):
    batches, local_rows, channels = query_in.shape
    context_size = lax.axis_size("context")
    seq_length = local_rows * context_size
    grad_scale = float(batches * seq_length * GROUP) ** (-0.5)
    margin = TAPS - 1
    tap_weights = jnp.repeat(short_filter, GROUP, axis=2)
    last_rows = jnp.stack(
        [
            query_in[:, local_rows - margin :],
            key_in[:, local_rows - margin :],
            value_in[:, local_rows - margin :],
        ]
    )
    before = shifted(last_rows, "context", 1)
    key_feat = featurize(key_in, before[1], tap_weights[1])
    value_feat = featurize(value_in, before[2], tap_weights[2])
    product = (key_feat * value_feat).astype(jnp.bfloat16)
    weight_rows = lax.all_gather(out_weight, "context", axis=0, tiled=True)
    band = make_band(long_filter)
    product_full = to_owners(product, "context")
    grad_full = gather_features(grad_out, "tensor")
    query_feat = featurize(query_in, before[0], tap_weights[0])
    conv_out = from_owners(
        correlation_call(forward_kernel, "conv_forward", band, product_full), "context"
    )
    gated = (query_feat * conv_out.astype(jnp.float32)).astype(jnp.bfloat16)
    gated, weight_rows = lax.optimization_barrier((gated, weight_rows))
    grad_acc = jnp.einsum("blo,oc->blc", grad_full, weight_rows, preferred_element_type=jnp.float32)
    grad_conv = (grad_acc * query_feat).astype(jnp.bfloat16)
    grad_conv_full = to_owners(grad_conv, "context")
    grad_weight = lax.psum_scatter(
        jnp.einsum("blo,blc->oc", grad_full, gated, preferred_element_type=jnp.float32).astype(
            jnp.bfloat16
        ),
        "context",
        scatter_dimension=0,
        tiled=True,
    ).astype(jnp.float32)
    block_out = jnp.einsum("blc,oc->blo", gated, weight_rows, preferred_element_type=jnp.float32)
    mixed_out = scatter_features(block_out, "tensor")
    grad_product = from_owners(
        correlation_call(backward_kernel, "conv_backward", band, grad_conv_full), "context"
    )
    grad_long = long_grad_call(grad_conv_full, product_full, long_filter.shape[0], grad_scale)
    product_grad = grad_product.astype(jnp.float32)
    grad_qfeat = grad_acc * conv_out.astype(jnp.float32)
    grad_kfeat = product_grad * value_feat
    grad_vfeat = product_grad * key_feat
    first_rows = jnp.stack([grad_qfeat[:, :margin], grad_kfeat[:, :margin], grad_vfeat[:, :margin]])
    following = shifted(first_rows.astype(jnp.bfloat16), "context", -1).astype(first_rows.dtype)
    grad_query = unfeaturize(grad_qfeat, following[0], tap_weights[0]).astype(jnp.bfloat16)
    grad_key = unfeaturize(grad_kfeat, following[1], tap_weights[1]).astype(jnp.bfloat16)
    grad_value = unfeaturize(grad_vfeat, following[2], tap_weights[2]).astype(jnp.bfloat16)
    return (mixed_out, grad_query, grad_key, grad_value, grad_weight, grad_long)


def solution(mesh):
    in_specs = (
        P(None, "context", "tensor"),
        P(None, "context", "tensor"),
        P(None, "context", "tensor"),
        P(None, None, "tensor"),
        P(("tensor", "context"), None),
        P("context", "tensor"),
        P(None, "context", "tensor"),
    )
    out_specs = (
        P(None, "context", "tensor"),
        P(None, "context", "tensor"),
        P(None, "context", "tensor"),
        P(None, "context", "tensor"),
        P("context", "tensor"),
        P(("tensor", "context"), None),
    )
    return jax.shard_map(body, mesh=mesh, in_specs=in_specs, out_specs=out_specs, check_vma=False)
```

```python
import functools

import jax
import jax.numpy as jnp
from jax import lax
from jax.experimental import pallas as pl
from jax.experimental.pallas import tpu as pltpu
from jax.sharding import PartitionSpec as P

GROUP = 16
TAPS = 7
BLOCK = 256
HALF = 128
VMEM_LIMIT = 60 * 1024 * 1024


def shifted(value, axis, steps):
    count = lax.axis_size(axis)
    first, last = (max(0, -steps), min(count, count - steps))
    return lax.ppermute(value, axis, [(source, source + steps) for source in range(first, last)])


def whole_vmem(count):
    return [pl.BlockSpec(memory_space=pltpu.VMEM)] * count


def band_kernel(filter_ref, band_ref):
    groups, length = filter_ref.shape
    zeros = jnp.zeros((HALF, HALF), jnp.float32)

    def one_group(g, carry):
        row = jnp.broadcast_to(filter_ref[pl.ds(g, 1), :], (HALF, length))
        padded = jnp.concatenate([row, zeros], axis=1)
        rolled = pltpu.roll(padded, 0, 1, stride=1, stride_axis=0).astype(jnp.bfloat16)
        band_ref[g, 0:HALF, :] = rolled[:, :length]
        band_ref[g, HALF:BLOCK, :] = jnp.concatenate(
            [jnp.zeros((HALF, HALF), jnp.bfloat16), rolled[:, : length - HALF]], axis=1
        )
        return carry

    lax.fori_loop(0, groups, one_group, 0)


def make_band(long_filter):
    groups, length = long_filter.shape
    return pl.pallas_call(
        band_kernel,
        out_shape=jax.ShapeDtypeStruct((groups, BLOCK, length), jnp.bfloat16),
        in_specs=whole_vmem(1),
        out_specs=pl.BlockSpec(memory_space=pltpu.VMEM),
        compiler_params=pltpu.CompilerParams(vmem_limit_bytes=VMEM_LIMIT),
        cost_estimate=pl.CostEstimate(
            flops=0, bytes_accessed=groups * BLOCK * length * 2, transcendentals=0
        ),
        name="band",
    )(long_filter)


def exchange_matrix():
    row = lax.broadcasted_iota(jnp.int32, (BLOCK, BLOCK), 0)
    column = lax.broadcasted_iota(jnp.int32, (BLOCK, BLOCK), 1)
    return jnp.where(row + column == BLOCK - 1, 1.0, 0.0).astype(jnp.bfloat16)


def group_mask(g, rows, columns, channels):
    lane = lax.broadcasted_iota(jnp.int32, (rows, columns), 1)
    return (lane % channels) // GROUP == g


def correlate(band_ref, work_ref, total_ref, groups, channels):
    length, columns = work_ref.shape
    blocks = length // BLOCK
    total_ref[...] = jnp.zeros_like(total_ref)

    def one_group(g, carry):
        mask = group_mask(g, 1, columns, channels).astype(jnp.bfloat16)
        masked = work_ref[...] * mask
        for j in range(blocks):
            rows = slice(j * BLOCK, (j + 1) * BLOCK)
            total_ref[rows, :] += jnp.dot(
                band_ref[g, :, : (blocks - j) * BLOCK],
                masked[j * BLOCK :, :],
                preferred_element_type=jnp.float32,
            )
        return carry

    lax.fori_loop(0, groups, one_group, 0)


def load_block(source_ref, j):
    batches, local_rows, channels = source_ref.shape[1:]
    first, count = j * BLOCK // local_rows, BLOCK // local_rows
    return jnp.concatenate(
        [
            source_ref[first : first + count, b].reshape(BLOCK, channels)
            for b in range(batches)
        ],
        axis=1,
    )


def store_block(target_ref, j, value):
    batches, local_rows, channels = target_ref.shape[1:]
    first, count = j * BLOCK // local_rows, BLOCK // local_rows
    for b in range(batches):
        target_ref[first : first + count, b] = value[
            :, b * channels : (b + 1) * channels
        ].reshape(count, local_rows, channels)


def forward_kernel(band_ref, product_ref, out_ref, work_ref, total_ref):
    groups = band_ref.shape[0]
    length, channels = work_ref.shape[0], product_ref.shape[3]
    blocks = length // BLOCK
    exchange = exchange_matrix()
    for j in range(blocks):
        block = load_block(product_ref, j)
        mirror = slice((blocks - 1 - j) * BLOCK, (blocks - j) * BLOCK)
        work_ref[mirror, :] = jnp.dot(
            exchange, block, preferred_element_type=jnp.float32
        ).astype(jnp.bfloat16)
    correlate(band_ref, work_ref, total_ref, groups, channels)
    for j in range(blocks):
        mirror = slice((blocks - 1 - j) * BLOCK, (blocks - j) * BLOCK)
        rounded = total_ref[mirror, :].astype(jnp.bfloat16)
        value = jnp.dot(exchange, rounded, preferred_element_type=jnp.float32)
        store_block(out_ref, j, value.astype(jnp.bfloat16))


def backward_kernel(band_ref, grad_ref, out_ref, work_ref, total_ref):
    groups = band_ref.shape[0]
    length, channels = work_ref.shape[0], grad_ref.shape[3]
    blocks = length // BLOCK
    for j in range(blocks):
        rows = slice(j * BLOCK, (j + 1) * BLOCK)
        work_ref[rows, :] = load_block(grad_ref, j)
    correlate(band_ref, work_ref, total_ref, groups, channels)
    for j in range(blocks):
        rows = slice(j * BLOCK, (j + 1) * BLOCK)
        store_block(out_ref, j, total_ref[rows, :].astype(jnp.bfloat16))


def long_grad_kernel(scale, grad_ref, product_ref, out_ref, grad_work, product_work, sums):
    groups, length = out_ref.shape
    channels = grad_ref.shape[3]
    blocks = length // BLOCK
    wide = grad_work.shape[1] // blocks
    exchange = exchange_matrix()
    for j in range(blocks):
        columns = slice(j * wide, (j + 1) * wide)
        grad_work[:, columns] = load_block(grad_ref, j)
        product_work[:, columns] = jnp.dot(
            exchange, load_block(product_ref, j), preferred_element_type=jnp.float32
        ).astype(jnp.bfloat16)
    sums[:, length:] = jnp.zeros_like(sums[:, length:])

    def one_group(g, carry):
        mask = group_mask(g, 1, blocks * wide, channels).astype(jnp.bfloat16)
        masked = product_work[...] * mask
        for d in range(blocks):
            sums[:, d * BLOCK : (d + 1) * BLOCK] = lax.dot_general(
                grad_work[:, d * wide :],
                masked[:, : (blocks - d) * wide],
                (((1,), (1,)), ((), ())),
                preferred_element_type=jnp.float32,
            )
        low = sums[0:HALF, :]
        high = sums[HALF:BLOCK, :]
        folded = low + jnp.concatenate(
            [jnp.zeros((HALF, HALF), jnp.float32), high[:, : length + BLOCK - HALF]], axis=1
        )
        rolled = pltpu.roll(folded, 0, 1, stride=1, stride_axis=0)
        summed = jnp.sum(rolled, axis=0, keepdims=True)
        placed = pltpu.roll(
            jnp.broadcast_to(summed, (8, length + BLOCK)), length + 1, 1
        )
        out_ref[pl.ds(g, 1), :] = placed[0:1, :length] * scale
        return carry

    lax.fori_loop(0, groups, one_group, 0)


def correlation_call(kernel, name, band, signal):
    owners, batches, local_rows, channels = signal.shape
    length = owners * local_rows
    groups = band.shape[0]
    columns = batches * channels
    return pl.pallas_call(
        kernel,
        out_shape=jax.ShapeDtypeStruct(signal.shape, jnp.bfloat16),
        in_specs=whole_vmem(2),
        out_specs=pl.BlockSpec(memory_space=pltpu.VMEM),
        scratch_shapes=[
            pltpu.VMEM((length, columns), jnp.bfloat16),
            pltpu.VMEM((length, columns), jnp.float32),
        ],
        compiler_params=pltpu.CompilerParams(vmem_limit_bytes=VMEM_LIMIT),
        cost_estimate=pl.CostEstimate(
            flops=groups * length * length * columns,
            bytes_accessed=band.size * 2 + signal.size * 4,
            transcendentals=0,
        ),
        name=name,
    )(band, signal)


def long_grad_call(grad, product, groups, scale):
    owners, batches, local_rows, channels = grad.shape
    length = owners * local_rows
    blocks = length // BLOCK
    columns = batches * channels
    return pl.pallas_call(
        functools.partial(long_grad_kernel, scale),
        out_shape=jax.ShapeDtypeStruct((groups, length), jnp.float32),
        in_specs=whole_vmem(2),
        out_specs=pl.BlockSpec(memory_space=pltpu.VMEM),
        scratch_shapes=[
            pltpu.VMEM((BLOCK, blocks * columns), jnp.bfloat16),
            pltpu.VMEM((BLOCK, blocks * columns), jnp.bfloat16),
            pltpu.VMEM((BLOCK, length + BLOCK), jnp.float32),
        ],
        compiler_params=pltpu.CompilerParams(vmem_limit_bytes=VMEM_LIMIT),
        cost_estimate=pl.CostEstimate(
            flops=groups * length * length * columns,
            bytes_accessed=grad.size * 4 + groups * length * 4,
            transcendentals=0,
        ),
        name="long_grad",
    )(grad, product)


def featurize(signal, leading, tap_weights):
    local_rows = signal.shape[1]
    padded = jnp.concatenate([leading, signal], axis=1)
    summed = jnp.zeros(signal.shape, jnp.float32)
    for offset in range(TAPS):
        lead_at = TAPS - 1 - offset
        summed = summed + tap_weights[offset] * padded[:, lead_at : lead_at + local_rows].astype(
            jnp.float32
        )
    return summed


def unfeaturize(gradient, trailing, tap_weights):
    local_rows = gradient.shape[1]
    padded = jnp.concatenate([gradient, trailing], axis=1)
    summed = jnp.zeros(gradient.shape, jnp.float32)
    for offset in range(TAPS):
        summed = summed + tap_weights[offset] * padded[:, offset : offset + local_rows]
    return summed


def to_owners(value, axis):
    count = lax.axis_size(axis)
    batches, rows, channels = value.shape
    split = value.reshape(batches, rows, count, channels // count).transpose(2, 0, 1, 3)
    return lax.all_to_all(split, axis, split_axis=0, concat_axis=0, tiled=True)


def from_owners(value, axis):
    owners, batches, rows, channels = value.shape
    back = lax.all_to_all(value, axis, split_axis=0, concat_axis=0, tiled=True)
    return back.transpose(1, 2, 0, 3).reshape(batches, rows, owners * channels)


def gather_features(value, axis):
    count = lax.axis_size(axis)
    me = lax.axis_index(axis)
    width = value.shape[2]
    gathered = jnp.zeros(value.shape[:2] + (count * width,), value.dtype)
    for step in range(count):
        part = value
        if step:
            pairs = [(source, (source - step) % count) for source in range(count)]
            part = lax.ppermute(value, axis, pairs)
        gathered = lax.dynamic_update_slice_in_dim(
            gathered, part, (me + step) % count * width, 2
        )
    return gathered


def scatter_features(value, axis):
    count = lax.axis_size(axis)
    me = lax.axis_index(axis)
    width = value.shape[2] // count
    total = lax.dynamic_slice_in_dim(value, me * width, width, 2).astype(jnp.float32)
    for step in range(1, count):
        part = lax.dynamic_slice_in_dim(value, (me + step) % count * width, width, 2)
        pairs = [(source, (source + step) % count) for source in range(count)]
        total = total + lax.ppermute(part.astype(jnp.bfloat16), axis, pairs).astype(jnp.float32)
    return total.astype(jnp.bfloat16)


def ring_order(chips):
    return list(range(0, chips, 2)) + list(range(chips - 1, 0, -2))


def ring_pairs(order, step):
    chips = len(order)
    return [
        (2 * order[k] + core, 2 * order[(k + step) % chips] + core)
        for k in range(chips)
        for core in range(2)
    ]


def scattered_weight_grad(grad_full, gated, axis):
    count = lax.axis_size(axis)
    chips = count // 2
    order = ring_order(chips)
    me = lax.axis_index(axis)
    core = me % 2
    place = jnp.array([order.index(chip) for chip in range(chips)], jnp.int32)[me // 2]
    order_table = jnp.array(order, jnp.int32)
    rows = grad_full.shape[2] // count
    half = gated.shape[2] // 2
    halves = (gated[:, :, :half], gated[:, :, half:])
    siblings = [(device, device ^ 1) for device in range(count)]

    def partial_sum(position, owner_core, side):
        owner = 2 * order_table[position % chips] + owner_core
        columns = lax.dynamic_slice_in_dim(grad_full, owner * rows, rows, 2)
        return jnp.einsum(
            "blo,blc->oc", columns, halves[side], preferred_element_type=jnp.float32
        )

    def positions(step):
        return (place - 1 - step, place + 1 + step)

    received = []
    for step in range(chips):
        sent = jnp.stack(
            [
                partial_sum(positions(step)[side], 1 - core, side).astype(jnp.bfloat16)
                for side in range(2)
            ]
        )
        received.append(lax.ppermute(sent, axis, siblings))
    travelling = [None, None]
    for step in range(chips):
        for side in range(2):
            total = partial_sum(positions(step)[side], core, side)
            total = total + received[step][side].astype(jnp.float32)
            if step:
                total = total + travelling[side].astype(jnp.float32)
            if step < chips - 1:
                total = lax.ppermute(
                    total.astype(jnp.bfloat16), axis, ring_pairs(order, 1 - 2 * side)
                )
            travelling[side] = total
    return jnp.concatenate(travelling, axis=1)


def body(query_in, key_in, value_in, short_filter, long_filter, out_weight, grad_out):
    batches, local_rows, channels = query_in.shape
    context_size = lax.axis_size("context")
    seq_length = local_rows * context_size
    grad_scale = float(batches * seq_length * GROUP) ** (-0.5)
    margin = TAPS - 1
    tap_weights = jnp.repeat(short_filter, GROUP, axis=2)
    last_rows = jnp.stack(
        [
            query_in[:, local_rows - margin :],
            key_in[:, local_rows - margin :],
            value_in[:, local_rows - margin :],
        ]
    )
    before = shifted(last_rows, "context", 1)
    key_feat = featurize(key_in, before[1], tap_weights[1])
    value_feat = featurize(value_in, before[2], tap_weights[2])
    product = (key_feat * value_feat).astype(jnp.bfloat16)
    weight_rows = lax.all_gather(out_weight, "context", axis=0, tiled=True)
    band = make_band(long_filter)
    product_full = to_owners(product, "context")
    grad_full = gather_features(grad_out, "tensor")
    product_full, grad_full = lax.optimization_barrier((product_full, grad_full))
    query_feat = featurize(query_in, before[0], tap_weights[0])
    conv_out = from_owners(
        correlation_call(forward_kernel, "conv_forward", band, product_full), "context"
    )
    gated = (query_feat * conv_out.astype(jnp.float32)).astype(jnp.bfloat16)
    gated, weight_rows = lax.optimization_barrier((gated, weight_rows))
    grad_acc = jnp.einsum("blo,oc->blc", grad_full, weight_rows, preferred_element_type=jnp.float32)
    grad_conv = (grad_acc * query_feat).astype(jnp.bfloat16)
    grad_conv, gated = lax.optimization_barrier((grad_conv, gated))
    grad_conv_full = to_owners(grad_conv, "context")
    grad_weight = scattered_weight_grad(grad_full, gated, "context")
    block_out = jnp.einsum("blc,oc->blo", gated, weight_rows, preferred_element_type=jnp.float32)
    mixed_out = scatter_features(block_out, "tensor")
    grad_product = from_owners(
        correlation_call(backward_kernel, "conv_backward", band, grad_conv_full), "context"
    )
    grad_long = long_grad_call(grad_conv_full, product_full, long_filter.shape[0], grad_scale)
    product_grad = grad_product.astype(jnp.float32)
    grad_qfeat = grad_acc * conv_out.astype(jnp.float32)
    grad_kfeat = product_grad * value_feat
    grad_vfeat = product_grad * key_feat
    first_rows = jnp.stack([grad_qfeat[:, :margin], grad_kfeat[:, :margin], grad_vfeat[:, :margin]])
    following = shifted(first_rows.astype(jnp.bfloat16), "context", -1).astype(first_rows.dtype)
    grad_query = unfeaturize(grad_qfeat, following[0], tap_weights[0]).astype(jnp.bfloat16)
    grad_key = unfeaturize(grad_kfeat, following[1], tap_weights[1]).astype(jnp.bfloat16)
    grad_value = unfeaturize(grad_vfeat, following[2], tap_weights[2]).astype(jnp.bfloat16)
    return (mixed_out, grad_query, grad_key, grad_value, grad_weight, grad_long)


def solution(mesh):
    in_specs = (
        P(None, "context", "tensor"),
        P(None, "context", "tensor"),
        P(None, "context", "tensor"),
        P(None, None, "tensor"),
        P(("tensor", "context"), None),
        P("context", "tensor"),
        P(None, "context", "tensor"),
    )
    out_specs = (
        P(None, "context", "tensor"),
        P(None, "context", "tensor"),
        P(None, "context", "tensor"),
        P(None, "context", "tensor"),
        P("context", "tensor"),
        P(("tensor", "context"), None),
    )
    return jax.shard_map(body, mesh=mesh, in_specs=in_specs, out_specs=out_specs, check_vma=False)
```
